32 devices in a mesh: region: 8 (over y, x, core), tm: 4 (over z).
Axes of the slice: x: 2, y: 2, z: 4, core: 2. Of those that a mesh axis runs over, the one named last changes fastest.
Arguments:
- jacobian: bfloat16 [24576, 2048], P(('region', 'tm')), may hold values from -0.375 to 0.375
- foot_block: int32 [24576], P(('region', 'tm')), may hold values from 0 to 63, as said below
- foot_time: int32 [24576], P(('region', 'tm')), may hold values from 0 to 208, as said below
- obs_weight: bfloat16 [24576], P(('region', 'tm')), may hold values from 0.29882812 to 3
- misfit: bfloat16 [24576], P(('region', 'tm')), may hold values from -6 to 6
- kept_list: int32 [16384], P(('region', 'tm')), may hold values from 0 to 767, as said below
- kept_count: int32 [32], P(('region', 'tm')), may hold values from 256 to 512, as said below
- prior_std: float32 [224, 64, 128], P('tm', 'region'), may hold values from 0.4 to 11
- time_factor: float32 [224, 224], replicated, may hold values from -0.3 to 1.3
Outputs:
- solution: float32 [224, 64, 128], P('tm', 'region')
- residual: float32 [224, 64, 128], P('tm', 'region')
The draws below stay inside these ranges and needn't reach their ends.
Inputs may be any that keep to these rules, and one draw needn't show every extreme that they name: `kept_list`: the 512 entries of one device are distinct row numbers within that device's own 768 rows. A device keeps the rows named by the first kept_count entries of its list. Region block of the footprint; the block is owned by the region index foot_block // 8. A footprint covers steps foot_time to foot_time + 15, all in the time window foot_time // 56: foot_time % 56 <= 40. Among the kept rows of one device, at most 24 have footprints owned by any one device (region index foot_block // 8, time index foot_time // 56); in every draw some owning device gets exactly 24 kept rows from every device.
All inputs are finite; a program needn't handle non-finite values.
Results may differ from the reference program's by a relative error of at most 0.0004.
Values may be sent and summed in bfloat16 or wider, within the bound.
No kernel may reach another device: no remote copies, remote signals or barrier semaphores. Data moves between devices by JAX's collectives and lax.ppermute only.
A program may use at most 128 MiB of HBM per device.

```python
import math
import jax
import jax.numpy as jnp
from jax import lax

CELLS = 128
REG_DEV = 8
TDEV = 56
LAG = 16
KEEP = 512
ITERS = 2
POOL = 768
CAP = 24
REGIONS = 64
NT = 224
N_REGION = 8
N_TM = 4


def sounding_plan(key):
    key = jax.random.fold_in(key, 31)
    devices = N_REGION * N_TM
    capacity = CAP
    key_heavy, key_count, key_full, key_low, key_rows = jax.random.split(key, 5)
    heavy = jax.random.randint(key_heavy, (), 0, devices)

    def one_device(sub):
        parts = jax.random.split(sub, 8)
        order = jax.random.permutation(parts[0], POOL)[:KEEP].astype(jnp.int32)
        spots = jax.random.permutation(parts[1], (devices - 1) * capacity)[:KEEP - capacity].astype(jnp.int32)
        others = spots // capacity
        others = others + (others >= heavy).astype(jnp.int32)
        target = jnp.concatenate([jnp.full((capacity,), heavy, jnp.int32), others])
        shuffle = jax.random.permutation(parts[2], KEEP // 2)
        target = jnp.concatenate([target[:KEEP // 2][shuffle], target[KEEP // 2:]])
        inside = jax.random.randint(parts[3], (KEEP,), 0, REG_DEV)
        offset = jax.random.randint(parts[4], (KEEP,), 0, TDEV - LAG + 1)
        blocks = target // N_TM * REG_DEV + inside
        starts = target % N_TM * TDEV + offset
        pool_blocks = jax.random.randint(parts[5], (POOL,), 0, REGIONS)
        pool_starts = jax.random.randint(parts[6], (POOL,), 0, N_TM) * TDEV + jax.random.randint(parts[7], (POOL,), 0, TDEV - LAG + 1)
        pool_blocks = pool_blocks.at[order].set(blocks)
        pool_starts = pool_starts.at[order].set(starts)
        return (order, pool_blocks.astype(jnp.int32), pool_starts.astype(jnp.int32))
    lists, blocks, starts = jax.vmap(one_device)(jax.random.split(key_rows, devices))
    counts = jax.random.randint(key_count, (devices,), KEEP // 2, KEEP + 1)
    full_at = jax.random.randint(key_full, (), 0, devices)
    low_at = (full_at + 1 + jax.random.randint(key_low, (), 0, devices - 1)) % devices
    counts = counts.at[full_at].set(KEEP).at[low_at].set(KEEP // 2)
    return (lists.reshape(-1), counts.astype(jnp.int32), blocks.reshape(-1), starts.reshape(-1))


def draw_kept_list(key, part):
    return sounding_plan(key)[0]


def draw_kept_count(key, part):
    return sounding_plan(key)[1]


def draw_foot_block(key, part):
    return sounding_plan(key)[2]


def draw_foot_time(key, part):
    return sounding_plan(key)[3]


def draw_prior_std(key, part):
    key = jax.random.fold_in(key, 57)
    ramp = 3.0 ** (jnp.arange(REGIONS, dtype=jnp.float32) / REGIONS)
    shape = (NT, REGIONS, CELLS)
    base = jnp.exp(jax.random.uniform(key, shape, jnp.float32, math.log(0.4), math.log(1.2)))
    return base * ramp[None, :, None]


def draw_time_factor(key, part):
    key = jax.random.fold_in(key, 83)
    ident = (jnp.arange(NT)[:, None] == jnp.arange(NT)[None, :]).astype(jnp.float32)
    noise = jnp.clip(jax.random.normal(key, (NT, NT), jnp.float32), -3.0, 3.0)
    return ident + 0.5 / math.sqrt(NT) * noise


def block_scale(stream_key, dims, shards, low, high):
    def one(position, shards_of):
        steps = jax.random.uniform(jax.random.fold_in(jax.random.fold_in(stream_key, 6), position), (shards_of,), jnp.float32, low / len(shards), high / len(shards))
        return jnp.repeat(jnp.exp(steps), dims[position] // shards_of).reshape((-1,) + (1,) * (len(dims) - position - 1))

    loudness = one(*shards[0])
    for cut in shards[1:]:
        loudness = loudness * one(*cut)
    return loudness


def centred(own_key, shape, deviation, reach, shards=(), held_as=jnp.bfloat16):
    values = jax.random.normal(own_key, shape, jnp.float32) * deviation
    if len(shards) > 0:
        values = block_scale(own_key, shape, shards, -0.22, 0.18) * values
    return jnp.clip(values, min=-reach, max=reach).astype(held_as)


def setup_inputs(seed: int = 0) -> dict:
    keys = jax.random.split(jax.random.key(seed), 10)
    return {
        "jacobian": centred(keys[0], (N_REGION * N_TM * POOL, LAG * CELLS), (LAG * CELLS // 8) ** -0.5, 0.375, ((0, 32),)),
        "foot_block": draw_foot_block(jax.random.fold_in(keys[9], 71), 0),
        "foot_time": draw_foot_time(jax.random.fold_in(keys[9], 71), 0),
        "obs_weight": jnp.clip(jnp.exp(math.log(3.0) - 2.306499 * jax.random.uniform(keys[3], (N_REGION * N_TM * POOL,), jnp.float32) ** block_scale(keys[3], (N_REGION * N_TM * POOL,), ((0, 32),), -0.2, 0.2)), 0.29882812, 3.0).astype(jnp.bfloat16),
        "misfit": centred(keys[4], (N_REGION * N_TM * POOL,), 1.0, 6.0, ((0, 32),)),
        "kept_list": draw_kept_list(jax.random.fold_in(keys[9], 71), 0),
        "kept_count": draw_kept_count(jax.random.fold_in(keys[9], 71), 0),
        "prior_std": draw_prior_std(jax.random.fold_in(keys[9], 71), 0),
        "time_factor": draw_time_factor(jax.random.fold_in(keys[9], 71), 0),
    }


def reference(jacobian, foot_block, foot_time, obs_weight, misfit, kept_list, kept_count, prior_std, time_factor):
    flat_shape = (NT * REGIONS, CELLS)
    offsets = jnp.arange(LAG, dtype=jnp.int32)

    def sounding_pass(field, with_field):
        flat = field.reshape(flat_shape)

        def visit(total, device):
            selected = lax.dynamic_slice_in_dim(kept_list, device * KEEP, KEEP, 0).astype(jnp.int32) + (device * POOL).astype(jnp.int32)
            shaped = jacobian[selected].astype(jnp.float32).reshape(KEEP, LAG, CELLS)
            index = (foot_time[selected][:, None].astype(jnp.int32) + offsets[None, :]) * REGIONS + foot_block[selected][:, None].astype(jnp.int32)
            kept_now = jnp.arange(KEEP, dtype=jnp.int32) < kept_count[device]
            weight = jnp.where(kept_now, obs_weight[selected].astype(jnp.float32), jnp.zeros((KEEP,), jnp.float32))
            if with_field:
                values = weight * jnp.sum(shaped * flat[index], axis=(1, 2))
            else:
                values = weight * misfit[selected].astype(jnp.float32)
            return total.at[index].add(shaped * values[:, None, None]), None

        total = lax.scan(visit, jnp.zeros(flat_shape, jnp.float32), jnp.arange(N_REGION * N_TM, dtype=jnp.int32))[0]
        return total.reshape(NT, REGIONS, CELLS)

    def lower(field):
        mixed = jnp.dot(time_factor, field.reshape(NT, REGIONS * CELLS), precision=lax.Precision.HIGHEST)
        return prior_std * mixed.reshape(NT, REGIONS, CELLS)

    def upper(field):
        mixed = jnp.dot(time_factor.T, (prior_std * field).reshape(NT, REGIONS * CELLS), precision=lax.Precision.HIGHEST)
        return mixed.reshape(NT, REGIONS, CELLS)

    def operator(field):
        return field + upper(sounding_pass(lower(field), True))

    rhs = upper(sounding_pass(prior_std, False))
    solution = jnp.zeros_like(rhs)
    residual = rhs
    direction = rhs
    norm_now = jnp.sum(residual * residual)
    for iteration in range(ITERS):
        image = operator(direction)
        alpha = norm_now / jnp.sum(direction * image)
        solution = solution + alpha * direction
        residual = residual - alpha * image
        norm_next = jnp.sum(residual * residual)
        direction = residual + (norm_next / norm_now) * direction
        norm_now = norm_next
    return solution, residual
```

```python
import functools

import jax
import jax.numpy as jnp
from jax import lax
from jax.experimental import pallas as pl
from jax.experimental.pallas import tpu as pltpu
from jax.sharding import PartitionSpec as P

F32 = jnp.float32
BF16 = jnp.bfloat16
LANES = 128
VMEM_LIMIT = 40 << 20
META = 8


class Dims:
    def __init__(self, jacobian, kept_list, prior_std, regions, windows):
        self.regions = regions
        self.windows = windows
        self.devices = regions * windows
        self.time_dev, self.blocks, self.cells = prior_std.shape
        self.pool = jacobian.shape[0]
        self.keep = kept_list.shape[0]
        self.lag = jacobian.shape[1] // self.cells
        self.times = self.time_dev * windows
        self.cap = 3 * self.keep // (2 * self.devices)
        self.slice = self.cells // windows
        self.group = LANES // self.slice
        self.tiles = self.lag // self.group
        self.width = self.lag * self.slice
        self.slots = self.devices * self.cap
        self.piece = windows * self.cap
        self.rows = self.piece + META
        self.offsets = -(-(self.time_dev - self.lag + 1) // 16) * 16
        self.places = self.offsets * self.blocks
        self.halves = self.blocks // self.group
        self.packed = self.halves * LANES
        assert self.cells == LANES and self.blocks == 8 and self.group == windows


def iota(shape, axis):
    return lax.broadcasted_iota(jnp.int32, shape, axis)


def onehot(match):
    return jnp.where(match, 1.0, 0.0).astype(BF16)


def dot(a, b, contract=(1, 0)):
    return lax.dot_general(
        a, b, (((contract[0],), (contract[1],)), ((), ())), preferred_element_type=F32
    )


def halves(x):
    high = x.astype(BF16)
    return high, (x - high.astype(F32)).astype(BF16)


def dot3(a, b):
    ah, al = halves(a)
    bh, bl = halves(b)
    return dot(ah, bh) + (dot(ah, bl) + dot(al, bh))


def group_of(shape, d):
    return iota(shape, 1) >> (d.slice.bit_length() - 1)


def everywhere(x, d):
    shift = LANES // 2
    while shift >= d.slice:
        x = x + pltpu.roll(x, shift, 1)
        shift //= 2
    return x


def params(**kw):
    return pltpu.CompilerParams(vmem_limit_bytes=VMEM_LIMIT, **kw)


def vmem():
    return pl.BlockSpec(memory_space=pltpu.VMEM)


def smem():
    return pl.BlockSpec(memory_space=pltpu.SMEM)


def pack_body(d, count_ref, list_ref, block_ref, time_ref, weight_ref, misfit_ref, jac_ref,
              out_ref, select_ref, meta_ref):
    step = pl.program_id(0)

    @pl.when(step == 0)
    def _():
        listed = jnp.broadcast_to(list_ref[...], (d.pool, d.keep))
        live = iota((d.pool, d.keep), 1) < count_ref[0]
        hit = onehot((iota((d.pool, d.keep), 0) == listed) & live)
        kept = dot(jnp.ones((16, d.keep), BF16), hit, (1, 1))[0:1] > 0.5
        block = block_ref[...]
        time = time_ref[...]
        window = jnp.zeros_like(time)
        for w in range(1, d.windows):
            window += jnp.where(time >= w * d.time_dev, 1, 0)
        target = (block >> 3) * d.windows + window
        target = jnp.where(kept, target, -1)
        mine = iota((d.devices, d.pool), 0) == jnp.broadcast_to(target, (d.devices, d.pool))
        before = onehot(iota((d.pool, d.pool), 0) < iota((d.pool, d.pool), 1))
        ranks = dot(onehot(mine), before)
        rank = jnp.sum(jnp.where(mine, ranks, 0.0), axis=0, keepdims=True).astype(jnp.int32)
        slot = jnp.where(kept, target * d.cap + rank, -1)
        select = onehot(iota((d.slots, d.pool), 0) == jnp.broadcast_to(slot, (d.slots, d.pool)))
        select_ref[...] = select
        row = iota((16, d.pool), 0)
        fields = jnp.where(row == 0, (block & 7).astype(F32), 0.0)
        fields = jnp.where(row == 1, (time - window * d.time_dev).astype(F32), fields)
        fields = jnp.where(row == 2, weight_ref[...].astype(F32), fields)
        fields = jnp.where(row == 3, misfit_ref[...].astype(F32), fields)
        fields = jnp.where(row == 4, 1.0, fields)
        meta_ref[...] = dot(fields.astype(BF16), select, (1, 1))[0:META]

    wide = d.group * LANES
    a, b = iota((wide, wide), 0), iota((wide, wide), 1)
    bits = d.slice.bit_length() - 1
    cell = a & (LANES - 1)
    place = ((cell >> bits) << 7) + ((a >> 7) << bits) + (cell & (d.slice - 1))
    turn = onehot(place == b)
    rows = dot(select_ref[...], jac_ref[...]).astype(BF16)
    turned = dot(rows, turn).astype(BF16)
    for r in range(d.regions):
        low = r * d.piece
        shifted = pltpu.roll(meta_ref[...], (d.slots - low) % d.slots, 1)[:, :LANES]
        meta = jnp.where(step == 0, shifted, 0.0).astype(BF16)
        for j in range(d.windows):
            out_ref[r, j, 0:d.piece, :] = turned[low:low + d.piece, j * LANES:(j + 1) * LANES]
            out_ref[r, j, d.piece:d.rows, :] = meta


def pack(d, count, listed, block, time, weight, misfit, jacobian):
    wide = d.group * LANES
    whole = lambda n: pl.BlockSpec((1, n), lambda g: (0, 0))
    return pl.pallas_call(
        functools.partial(pack_body, d),
        name="pack",
        grid=(d.tiles,),
        in_specs=[smem(), whole(d.keep)] + [whole(d.pool)] * 4
        + [pl.BlockSpec((d.pool, wide), lambda g: (0, g))],
        out_specs=pl.BlockSpec((d.regions, d.windows, d.rows, LANES), lambda g: (0, 0, 0, g)),
        out_shape=jax.ShapeDtypeStruct((d.regions, d.windows, d.rows, d.width), BF16),
        scratch_shapes=[pltpu.VMEM((d.slots, d.pool), BF16), pltpu.VMEM((META, d.slots), F32)],
        compiler_params=params(),
    )(count, listed[None], block[None], time[None], weight[None], misfit[None], jacobian)


def prior_body(d, me_ref, prior_ref, out_ref):
    me = me_ref[0]
    lane = group_of((d.time_dev, LANES), d)
    for h in range(d.halves):
        rows = [prior_ref[pl.ds(h * d.group + m, d.time_dev, stride=d.blocks), :] for m in range(d.group)]
        for s in range(d.windows):
            to = me ^ s
            total = jnp.zeros((d.time_dev, LANES), F32)
            for m in range(d.group):
                turn = (m - to + d.group) % d.group * d.slice
                total = jnp.where(lane == m, pltpu.roll(rows[m], turn, 1), total)
            out_ref[s, :, h * LANES:(h + 1) * LANES] = total


def split_prior(d, me, prior):
    return pl.pallas_call(
        functools.partial(prior_body, d),
        name="split_prior",
        in_specs=[smem(), vmem()],
        out_specs=vmem(),
        out_shape=jax.ShapeDtypeStruct((d.windows, d.time_dev, d.packed), F32),
        compiler_params=params(),
    )(me, prior.reshape(d.time_dev * d.blocks, LANES))


def join_body(d, me_ref, *refs):
    pieces, outs = refs[:d.windows], refs[d.windows:]
    me = me_ref[0]
    lane = group_of((d.time_dev, LANES), d)
    for k, out_ref in enumerate(outs):
        for h in range(d.halves):
            tiles = [p[k, :, h * LANES:(h + 1) * LANES] for p in pieces]
            for m in range(d.group):
                total = jnp.zeros((d.time_dev, LANES), F32)
                for s in range(d.windows):
                    source = me ^ s
                    turn = (source - m + d.group) % d.group * d.slice
                    total = jnp.where(lane == source, pltpu.roll(tiles[s], turn, 1), total)
                out_ref[pl.ds(h * d.group + m, d.time_dev, stride=d.blocks), :] = total


def join(d, me, pieces):
    flat = jax.ShapeDtypeStruct((d.time_dev * d.blocks, LANES), F32)
    outs = pl.pallas_call(
        functools.partial(join_body, d),
        name="join",
        in_specs=[smem()] + [vmem()] * d.windows,
        out_specs=[vmem()] * 2,
        out_shape=[flat, flat],
        compiler_params=params(),
    )(me, *pieces)
    return tuple(o.reshape(d.time_dev, d.blocks, LANES) for o in outs)


FRONT = 8
CHUNK = 16


def transpose_rows(d, row):
    return jnp.broadcast_to(row, (LANES, d.slots)).T


def spread(d, values, rows_ref, place_t_ref, std_ref, sum_ref, field_ref, packed_ref):
    sum_ref[...] = jnp.zeros_like(sum_ref)
    for w in range(d.windows):
        high, low = halves(values[w:w + 1])
        place = place_t_ref[w]
        rows = rows_ref[w]
        total = dot(place * high, rows) + dot(place * low, rows)
        for g in range(d.tiles):
            start = (FRONT + w * d.time_dev + d.group * g) * d.blocks
            sum_ref[start:start + d.places, :] += total[:, g * LANES:(g + 1) * LANES]
    size = CHUNK * d.blocks
    lane = group_of((size, LANES), d)

    @pl.loop(0, d.times // CHUNK)
    def _(i):
        start = pl.multiple_of(i * size, size)
        x = sum_ref[pl.ds(start + FRONT * d.blocks, size), :]
        for m in range(1, d.group):
            x = jnp.where(lane == m, sum_ref[pl.ds(start + (FRONT - m) * d.blocks, size), :], x)
        field_ref[pl.ds(start, size), :] = everywhere(x, d) * std_ref[pl.ds(start, size), :]

    lane = group_of((d.times, LANES), d)
    for h in range(d.halves):
        x = field_ref[pl.ds(h * d.group, d.times, stride=d.blocks), :]
        for m in range(1, d.group):
            x = jnp.where(lane == m, field_ref[pl.ds(h * d.group + m, d.times, stride=d.blocks), :], x)
        packed_ref[:, h * LANES:(h + 1) * LANES] = x


def unpack(d, packed, field_ref):
    lane = group_of((d.times, LANES), d)
    for h in range(d.halves):
        tile = packed[:, h * LANES:(h + 1) * LANES]
        for m in range(d.group):
            x = everywhere(jnp.where(lane == m, tile, 0.0), d)
            field_ref[pl.ds(h * d.group + m, d.times, stride=d.blocks), :] = x


def observe(d, mix_ref, packed_ref, rows_ref, place_ref, std_ref, field_ref, high_ref, low_ref, out_ref):
    unpack(d, dot3(mix_ref[...], packed_ref[...]), field_ref)
    size = CHUNK * d.blocks
    tail = 2 * CHUNK * d.blocks
    field_ref[pl.ds(d.times * d.blocks, tail), :] = jnp.zeros((tail, LANES), F32)

    @pl.loop(0, d.times // CHUNK)
    def _(i):
        start = pl.multiple_of(i * size, size)
        field_ref[pl.ds(start, size), :] = field_ref[pl.ds(start, size), :] * std_ref[pl.ds(start, size), :]

    lane = group_of((size, LANES), d)

    @pl.loop(0, d.times // CHUNK + 1)
    def _(i):
        start = pl.multiple_of(i * size, size)
        x = field_ref[pl.ds(start, size), :]
        for m in range(1, d.group):
            x = jnp.where(lane == m, field_ref[pl.ds(start + m * d.blocks, size), :], x)
        high, low = halves(x)
        high_ref[pl.ds(start, size), :] = high
        low_ref[pl.ds(start, size), :] = low

    for w in range(d.windows):
        starts = [(w * d.time_dev + d.group * g) * d.blocks for g in range(d.tiles)]
        high = jnp.concatenate([high_ref[s:s + d.places, :] for s in starts], axis=1)
        low = jnp.concatenate([low_ref[s:s + d.places, :] for s in starts], axis=1)
        place = place_ref[w]
        product = rows_ref[w].astype(F32) * (dot(place, high) + dot(place, low))
        part = product[:, :LANES]
        for g in range(1, d.tiles):
            part = part + product[:, g * LANES:(g + 1) * LANES]
        out_ref[w:w + 1, :] = jnp.sum(part.T, axis=0, keepdims=True)


def work_shapes(d):
    return [
        pltpu.VMEM(((FRONT + d.times + CHUNK) * d.blocks, LANES), F32),
        pltpu.VMEM(((d.times + 2 * CHUNK) * d.blocks, LANES), F32),
        pltpu.VMEM(((d.times + CHUNK) * d.blocks, LANES), BF16),
        pltpu.VMEM(((d.times + CHUNK) * d.blocks, LANES), BF16),
    ]


def first_body(d, me_ref, got_ref, mix_ref, *refs):
    stds = refs[:d.windows]
    (rows_ref, place_t_ref, place_ref, std_ref, weight_ref, value_ref, packed_ref, seen_ref,
     wide_ref, stdp_ref, sum_ref, field_ref, high_ref, low_ref) = refs[d.windows:]
    me = me_ref[0]
    for s in range(d.devices):
        x = got_ref[s, 0:d.piece, :].astype(F32)
        for w in range(d.windows):
            wide_ref[w, s * d.cap:(s + 1) * d.cap, :] = x[w * d.cap:(w + 1) * d.cap, :]
    for w in range(d.windows):
        rows_ref[w] = wide_ref[w].astype(BF16)
    count = d.slots // LANES
    lane = iota((META, LANES), 1)
    meta = [[jnp.zeros((META, LANES), F32)] * count for _ in range(d.windows)]
    for s in range(d.devices):
        m = got_ref[s, d.piece:d.rows, 0:LANES].astype(F32)
        low, high = s * d.cap, (s + 1) * d.cap
        for w in range(d.windows):
            turned = pltpu.roll(m, (low - w * d.cap) % LANES, 1)
            for tile in range(low // LANES, (high - 1) // LANES + 1):
                here = (lane + tile * LANES >= low) & (lane + tile * LANES < high)
                meta[w][tile] = jnp.where(here, turned, meta[w][tile])
    for w in range(d.windows):
        fields = jnp.concatenate(meta[w], axis=1)
        key = jnp.where(fields[4:5] > 0.5, fields[1:2] * d.blocks + fields[0:1], -1.0)
        number = key.astype(jnp.int32)
        place_t_ref[w] = onehot(iota((d.places, d.slots), 0) == jnp.broadcast_to(number, (d.places, d.slots)))
        column = transpose_rows(d, key).astype(jnp.int32)
        for k in range(d.places // LANES):
            place_ref[w, :, k * LANES:(k + 1) * LANES] = onehot(iota((d.slots, LANES), 1) + k * LANES == column)
        weight_ref[w:w + 1, :] = fields[2:3]
        value_ref[w:w + 1, :] = fields[2:3] * fields[3:4]
    for s in range(d.windows):
        stdp_ref[pl.ds(pl.multiple_of((me ^ s) * d.time_dev, 8), d.time_dev), :] = stds[s][...]
    unpack(d, stdp_ref[...], std_ref)
    spread(d, value_ref[...], rows_ref, place_t_ref, std_ref, sum_ref, field_ref, packed_ref)
    observe(d, mix_ref, packed_ref, rows_ref, place_ref, std_ref, field_ref, high_ref, low_ref, seen_ref)


def first(d, me, got, mix, stds):
    per_slot = jax.ShapeDtypeStruct((d.windows, d.slots), F32)
    return pl.pallas_call(
        functools.partial(first_body, d),
        name="first",
        in_specs=[smem()] + [vmem()] * (2 + d.windows),
        out_specs=[vmem()] * 8,
        out_shape=[
            jax.ShapeDtypeStruct((d.windows, d.slots, d.width), BF16),
            jax.ShapeDtypeStruct((d.windows, d.places, d.slots), BF16),
            jax.ShapeDtypeStruct((d.windows, d.slots, d.places), BF16),
            jax.ShapeDtypeStruct((d.times * d.blocks, LANES), F32),
            per_slot,
            per_slot,
            jax.ShapeDtypeStruct((d.times, d.packed), F32),
            per_slot,
        ],
        scratch_shapes=[
            pltpu.VMEM((d.windows, d.slots, d.width), F32),
            pltpu.VMEM((d.times, d.packed), F32),
        ] + work_shapes(d),
        compiler_params=params(),
    )(me, got, mix, *stds)


def total_of(x):
    return jnp.sum(jnp.sum(x, axis=0, keepdims=True), axis=1, keepdims=True)


def write_moments(out_ref, numbers):
    row = iota((8, LANES), 0)
    x = jnp.zeros((8, LANES), F32)
    for k, number in enumerate(numbers):
        x = jnp.where(row == k, jnp.broadcast_to(number, (8, LANES)), x)
    out_ref[...] = x


def second_body(d, rows_ref, place_t_ref, place_ref, std_ref, mix_ref, weight_ref, value_ref, *refs):
    parts = refs[:d.windows]
    (next_ref, packed_ref, seen_ref, moment_ref, sum_ref, field_ref, high_ref, low_ref) = refs[d.windows:]
    seen = parts[0][...]
    for p in parts[1:]:
        seen = seen + p[...]
    next_ref[...] = weight_ref[...] * seen
    write_moments(moment_ref, [total_of(value_ref[...] * seen), total_of(next_ref[...] * seen)])
    spread(d, next_ref[...], rows_ref, place_t_ref, std_ref, sum_ref, field_ref, packed_ref)
    observe(d, mix_ref, packed_ref, rows_ref, place_ref, std_ref, field_ref, high_ref, low_ref, seen_ref)


def second(d, rows, place_t, place, std, mix, weight, value, parts):
    per_slot = jax.ShapeDtypeStruct((d.windows, d.slots), F32)
    return pl.pallas_call(
        functools.partial(second_body, d),
        name="second",
        in_specs=[vmem()] * (7 + d.windows),
        out_specs=[vmem()] * 4,
        out_shape=[
            per_slot,
            jax.ShapeDtypeStruct((d.times, d.packed), F32),
            per_slot,
            jax.ShapeDtypeStruct((8, LANES), F32),
        ],
        scratch_shapes=work_shapes(d),
        compiler_params=params(),
    )(rows, place_t, place, std, mix, weight, value, *parts)


def third_body(d, weight_ref, value_ref, before_ref, *refs):
    parts = refs[:d.windows]
    next_ref, moment_ref = refs[d.windows:]
    seen = parts[0][...]
    for p in parts[1:]:
        seen = seen + p[...]
    next_ref[...] = weight_ref[...] * seen
    old = before_ref[...]
    write_moments(
        moment_ref,
        [old[0:1], old[1:2], total_of(value_ref[...] * seen), total_of(next_ref[...] * seen)],
    )


def third(d, weight, value, before, parts):
    return pl.pallas_call(
        functools.partial(third_body, d),
        name="third",
        in_specs=[vmem()] * (3 + d.windows),
        out_specs=[vmem()] * 2,
        out_shape=[
            jax.ShapeDtypeStruct((d.windows, d.slots), F32),
            jax.ShapeDtypeStruct((8, LANES), F32),
        ],
        compiler_params=params(),
    )(weight, value, before, *parts)


def fourth_body(d, value_ref, rows_ref, place_t_ref, std_ref, packed_ref, sum_ref, field_ref):
    spread(d, value_ref[...], rows_ref, place_t_ref, std_ref, sum_ref, field_ref, packed_ref)


def fourth(d, value, rows, place_t, std):
    return pl.pallas_call(
        functools.partial(fourth_body, d),
        name="fourth",
        in_specs=[vmem()] * 4,
        out_specs=vmem(),
        out_shape=jax.ShapeDtypeStruct((d.times, d.packed), F32),
        scratch_shapes=work_shapes(d)[:2],
        compiler_params=params(),
    )(value, rows, place_t, std)


def last_body(d, me_ref, moment_ref, factor_ref, a_ref, b_ref, c_ref, out_ref, hold_ref):
    me = me_ref[0]
    m0, m1, m2, m3 = (moment_ref[k:k + 1, :] for k in range(4))
    alpha0 = m0 / (m0 + m1)
    p, q = 1.0 - alpha0, -alpha0
    norm = p * p * m0 + 2.0 * p * q * m1 + q * q * m2
    e = p + norm / m0
    cross = (e * e * m0 + 2.0 * e * q * m1 + q * q * m2) + (e * e * m1 + 2.0 * e * q * m2 + q * q * m3)
    alpha1 = norm / cross
    for h in range(d.halves):
        low, high = h * LANES, (h + 1) * LANES
        a, b, c = a_ref[:, low:high], b_ref[:, low:high], c_ref[:, low:high]
        x = (alpha0 + alpha1 * e) * a + (alpha1 * q) * b
        r = (p - alpha1 * e) * a + (q - alpha1 * (e + q)) * b - (alpha1 * q) * c
        for k, v in enumerate((x, r)):
            fh, fl = halves(factor_ref[...])
            vh, vl = halves(v)
            y = dot(fh, vh, (0, 0)) + (dot(fh, vl, (0, 0)) + dot(fl, vh, (0, 0)))
            hold_ref[k, :, low:high] = y
    for s in range(d.windows):
        start = pl.multiple_of((me ^ s) * d.time_dev, 8)
        for k in range(2):
            out_ref[s, k] = hold_ref[k, pl.ds(start, d.time_dev), :]


def last(d, me, moments, factor, a, b, c):
    return pl.pallas_call(
        functools.partial(last_body, d),
        name="last",
        in_specs=[smem()] + [vmem()] * 5,
        out_specs=vmem(),
        out_shape=jax.ShapeDtypeStruct((d.windows, 2, d.time_dev, d.packed), F32),
        scratch_shapes=[pltpu.VMEM((2, d.times, d.packed), F32)],
        compiler_params=params(),
    )(me, moments, factor, a, b, c)


def swap(x, axis, step):
    size = lax.axis_size(axis)
    return lax.ppermute(x, axis, [(k, k ^ step) for k in range(size)])


def share(d, x):
    return [x] + [swap(x, "tm", s) for s in range(1, d.windows)]


def local(
    jacobian,
    foot_block,
    foot_time,
    obs_weight,
    misfit,
    kept_list,
    kept_count,
    prior_std,
    time_factor,
):
    d = Dims(jacobian, kept_list, prior_std, lax.axis_size("region"), lax.axis_size("tm"))
    me = lax.axis_index("tm").astype(jnp.int32).reshape(1)
    mix = jnp.dot(time_factor, time_factor.T, precision=lax.Precision.HIGHEST)
    ours = split_prior(d, me, prior_std)
    stds = [ours[0]] + [swap(ours[s], "tm", s) for s in range(1, d.windows)]
    pieces = pack(d, kept_count, kept_list, foot_block, foot_time, obs_weight, misfit, jacobian)
    got = lax.all_to_all(
        pieces.reshape(d.devices, d.rows, d.width), ("region", "tm"), split_axis=0, concat_axis=0, tiled=True
    )
    rows, place_t, place, std, weight, value0, u0, seen0 = first(d, me, got, mix, stds)
    value1, u1, seen1, early = second(d, rows, place_t, place, std, mix, weight, value0, share(d, seen0))
    value2, moments = third(d, weight, value1, early, share(d, seen1))
    u2 = fourth(d, value2, rows, place_t, std)
    step = 1
    while step < d.regions:
        moments = moments + swap(moments, "region", step)
        step *= 2
    both = last(d, me, moments, time_factor, u0, u1, u2)
    parts = [both[0]] + [swap(both[s], "tm", s) for s in range(1, d.windows)]
    return join(d, me, parts)


def solution(mesh):
    return jax.shard_map(
        local,
        mesh=mesh,
        in_specs=(
            P(("region", "tm"), None),
            P(("region", "tm")),
            P(("region", "tm")),
            P(("region", "tm")),
            P(("region", "tm")),
            P(("region", "tm")),
            P(("region", "tm")),
            P("tm", "region", None),
            P(),
        ),
        out_specs=(P("tm", "region", None), P("tm", "region", None)),
        check_vma=False,
    )
```

```python
import functools

import jax
import jax.numpy as jnp
from jax import lax
from jax.experimental import pallas as pl
from jax.experimental.pallas import tpu as pltpu
from jax.sharding import PartitionSpec as P

F32 = jnp.float32
BF16 = jnp.bfloat16
LANES = 128
VMEM_LIMIT = 40 << 20
META = 8


class Dims:
    def __init__(self, jacobian, kept_list, prior_std, regions, windows):
        self.regions = regions
        self.windows = windows
        self.devices = regions * windows
        self.time_dev, self.blocks, self.cells = prior_std.shape
        self.pool = jacobian.shape[0]
        self.keep = kept_list.shape[0]
        self.lag = jacobian.shape[1] // self.cells
        self.times = self.time_dev * windows
        self.cap = 3 * self.keep // (2 * self.devices)
        self.slice = self.cells // windows
        self.group = LANES // self.slice
        self.tiles = self.lag // self.group
        self.width = self.lag * self.slice
        self.slots = self.devices * self.cap
        self.piece = windows * self.cap
        self.chunk = regions * self.cap
        self.rows = self.piece + META
        self.head = META * (self.keep // (self.tiles * LANES))
        self.offsets = -(-(self.time_dev - self.lag + 1) // 16) * 16
        self.places = self.offsets * self.blocks
        self.halves = self.blocks // self.group
        self.packed = self.halves * LANES
        assert self.cells == LANES and self.blocks == 8 and self.group == windows


def iota(shape, axis):
    return lax.broadcasted_iota(jnp.int32, shape, axis)


def onehot(match):
    return jnp.where(match, 1.0, 0.0).astype(BF16)


def dot(a, b, contract=(1, 0)):
    return lax.dot_general(
        a, b, (((contract[0],), (contract[1],)), ((), ())), preferred_element_type=F32
    )


def halves(x):
    high = x.astype(BF16)
    return high, (x - high.astype(F32)).astype(BF16)


def dot3(a, b):
    ah, al = halves(a)
    bh, bl = halves(b)
    return dot(ah, bh) + (dot(ah, bl) + dot(al, bh))


def group_of(shape, d):
    return iota(shape, 1) >> (d.slice.bit_length() - 1)


def everywhere(x, d):
    shift = LANES // 2
    while shift >= d.slice:
        x = x + pltpu.roll(x, shift, 1)
        shift //= 2
    return x


def params(**kw):
    return pltpu.CompilerParams(vmem_limit_bytes=VMEM_LIMIT, **kw)


def vmem():
    return pl.BlockSpec(memory_space=pltpu.VMEM)


def smem():
    return pl.BlockSpec(memory_space=pltpu.SMEM)


def turn_matrix(d, me):
    wide = d.group * LANES
    a, b = iota((wide, wide), 0), iota((wide, wide), 1)
    bits = d.slice.bit_length() - 1
    cell = a & (LANES - 1)
    place = (((cell >> bits) ^ me) << 7) + ((a >> 7) << bits) + (cell & (d.slice - 1))
    return onehot(place == b)


def slice_body(d, me_ref, count_ref, list_ref, block_ref, time_ref, weight_ref, misfit_ref, jac_ref, *refs):
    outs, (select_ref, meta_ref, turn_ref) = refs[:d.windows], refs[d.windows:]
    step = pl.program_id(0)

    @pl.when(step == 0)
    def _():
        listed = jnp.broadcast_to(list_ref[...].astype(F32), (LANES, d.keep)).T.astype(jnp.int32)
        for k in range(d.pool // LANES):
            select_ref[:, k * LANES:(k + 1) * LANES] = onehot(iota((d.keep, LANES), 1) + k * LANES == listed)
        block = block_ref[...]
        time = time_ref[...]
        window = jnp.zeros_like(time)
        for w in range(1, d.windows):
            window += jnp.where(time >= w * d.time_dev, 1, 0)
        row = iota((16, d.pool), 0)
        fields = jnp.where(row == 0, (block >> 3).astype(F32), 0.0)
        fields = jnp.where(row == 1, window.astype(F32), fields)
        fields = jnp.where(row == 2, (block & 7).astype(F32), fields)
        fields = jnp.where(row == 3, (time - window * d.time_dev).astype(F32), fields)
        fields = jnp.where(row == 4, weight_ref[...].astype(F32), fields)
        fields = jnp.where(row == 5, misfit_ref[...].astype(F32), fields)
        fields = dot(fields.astype(BF16), select_ref[...], (1, 1))[0:META]
        live = (iota((META, d.keep), 1) < count_ref[0]) & (iota((META, d.keep), 0) == 6)
        meta_ref[...] = jnp.where(live, 1.0, fields).astype(BF16)
        turn_ref[...] = turn_matrix(d, me_ref[0])

    rows = dot(select_ref[...], jac_ref[...]).astype(BF16)
    turned = dot(rows, turn_ref[...]).astype(BF16)
    for s in range(d.windows):
        outs[s][0:d.keep, :] = turned[:, s * LANES:(s + 1) * LANES]
    per = d.keep // d.tiles
    for g in range(d.tiles):
        @pl.when(step == g)
        def _():
            meta = meta_ref[:, g * per:(g + 1) * per]
            for s in range(d.windows):
                outs[s][d.keep:d.keep + META * (per // LANES), :] = jnp.concatenate(
                    [meta[:, k * LANES:(k + 1) * LANES] for k in range(per // LANES)], axis=0
                )


def slice_rows(d, me, count, listed, block, time, weight, misfit, jacobian):
    wide = d.group * LANES
    whole = lambda n: pl.BlockSpec((1, n), lambda g: (0, 0))
    rows = d.keep + d.head
    return pl.pallas_call(
        functools.partial(slice_body, d),
        name="slice_rows",
        grid=(d.tiles,),
        in_specs=[smem(), smem(), whole(d.keep)] + [whole(d.pool)] * 4
        + [pl.BlockSpec((d.pool, wide), lambda g: (0, g))],
        out_specs=[pl.BlockSpec((rows, LANES), lambda g: (0, g))] * d.windows,
        out_shape=[jax.ShapeDtypeStruct((rows, d.width), BF16)] * d.windows,
        scratch_shapes=[
            pltpu.VMEM((d.keep, d.pool), BF16),
            pltpu.VMEM((META, d.keep), BF16),
            pltpu.VMEM((wide, wide), BF16),
        ],
        compiler_params=params(),
    )(me, count, listed[None], block[None], time[None], weight[None], misfit[None], jacobian)


def route_body(d, row_ref, in_ref, *outs):
    per = d.head // META
    meta = jnp.concatenate(
        [in_ref[d.keep + META * k:d.keep + META * (k + 1), g * LANES:(g + 1) * LANES]
         for g in range(d.tiles) for k in range(per)],
        axis=1,
    )
    fields = meta.astype(F32)
    region = fields[0:1].astype(jnp.int32) ^ row_ref[0]
    target = region * d.windows + fields[1:2].astype(jnp.int32)
    target = jnp.where(fields[6:7] > 0.5, target, -1)
    mine = iota((d.devices, d.keep), 0) == jnp.broadcast_to(target, (d.devices, d.keep))
    before = onehot(iota((d.keep, d.keep), 0) < iota((d.keep, d.keep), 1))
    ranks = dot(onehot(mine), before)
    rank = jnp.sum(jnp.where(mine, ranks, 0.0), axis=0, keepdims=True).astype(jnp.int32)
    slot = jnp.where(target >= 0, target * d.cap + rank, -1)
    select = onehot(iota((d.slots, d.keep), 0) == jnp.broadcast_to(slot, (d.slots, d.keep)))
    packed = dot(select, in_ref[0:d.keep, :]).astype(BF16)
    placed = dot(jnp.concatenate([meta, meta], axis=0), select, (1, 1))[0:META]
    for r in range(d.regions):
        low = r * d.piece
        outs[r][0:d.piece, :] = packed[low:low + d.piece]
        shifted = pltpu.roll(placed, (d.slots - low) % d.slots, 1)[:, :LANES]
        outs[r][d.piece:d.rows, 0:LANES] = shifted.astype(BF16)
        outs[r][d.piece:d.rows, LANES:] = jnp.zeros((META, d.width - LANES), BF16)


def route(d, row, piece):
    return pl.pallas_call(
        functools.partial(route_body, d),
        name="route",
        in_specs=[smem(), vmem()],
        out_specs=[vmem()] * d.regions,
        out_shape=[jax.ShapeDtypeStruct((d.rows, d.width), BF16)] * d.regions,
        compiler_params=params(),
    )(row, piece)


def prior_body(d, me_ref, prior_ref, *outs):
    me = me_ref[0]
    lane = group_of((d.time_dev, LANES), d)
    for h in range(d.halves):
        rows = [prior_ref[pl.ds(h * d.group + m, d.time_dev, stride=d.blocks), :] for m in range(d.group)]
        for s in range(d.windows):
            to = me ^ s
            total = jnp.zeros((d.time_dev, LANES), F32)
            for m in range(d.group):
                turn = (m - to + d.group) % d.group * d.slice
                total = jnp.where(lane == m, pltpu.roll(rows[m], turn, 1), total)
            outs[s][:, h * LANES:(h + 1) * LANES] = total


def split_prior(d, me, prior):
    return pl.pallas_call(
        functools.partial(prior_body, d),
        name="split_prior",
        in_specs=[smem(), vmem()],
        out_specs=[vmem()] * d.windows,
        out_shape=[jax.ShapeDtypeStruct((d.time_dev, d.packed), F32)] * d.windows,
        compiler_params=params(),
    )(me, prior.reshape(d.time_dev * d.blocks, LANES))


def join_body(d, me_ref, *refs):
    pieces, outs = refs[:d.windows], refs[d.windows:]
    me = me_ref[0]
    lane = group_of((d.time_dev, LANES), d)
    for k, out_ref in enumerate(outs):
        for h in range(d.halves):
            tiles = [p[k, :, h * LANES:(h + 1) * LANES] for p in pieces]
            for m in range(d.group):
                total = jnp.zeros((d.time_dev, LANES), F32)
                for s in range(d.windows):
                    source = me ^ s
                    turn = (source - m + d.group) % d.group * d.slice
                    total = jnp.where(lane == source, pltpu.roll(tiles[s], turn, 1), total)
                out_ref[pl.ds(h * d.group + m, d.time_dev, stride=d.blocks), :] = total


def join(d, me, pieces):
    flat = jax.ShapeDtypeStruct((d.time_dev * d.blocks, LANES), F32)
    outs = pl.pallas_call(
        functools.partial(join_body, d),
        name="join",
        in_specs=[smem()] + [vmem()] * d.windows,
        out_specs=[vmem()] * 2,
        out_shape=[flat, flat],
        compiler_params=params(),
    )(me, *pieces)
    return tuple(o.reshape(d.time_dev, d.blocks, LANES) for o in outs)


FRONT = 8
CHUNK = 16


def transpose_rows(d, row):
    return jnp.broadcast_to(row, (LANES, d.slots)).T


def spread(d, values, rows_ref, place_t_ref, std_ref, sum_ref, field_ref, packed_ref):
    sum_ref[...] = jnp.zeros_like(sum_ref)
    for w in range(d.windows):
        high, low = halves(values[w:w + 1])
        place = place_t_ref[w]
        rows = rows_ref[w]
        total = dot(place * high, rows) + dot(place * low, rows)
        for g in range(d.tiles):
            start = (FRONT + w * d.time_dev + d.group * g) * d.blocks
            sum_ref[start:start + d.places, :] += total[:, g * LANES:(g + 1) * LANES]
    size = CHUNK * d.blocks
    lane = group_of((size, LANES), d)

    @pl.loop(0, d.times // CHUNK)
    def _(i):
        start = pl.multiple_of(i * size, size)
        x = sum_ref[pl.ds(start + FRONT * d.blocks, size), :]
        for m in range(1, d.group):
            x = jnp.where(lane == m, sum_ref[pl.ds(start + (FRONT - m) * d.blocks, size), :], x)
        field_ref[pl.ds(start, size), :] = everywhere(x, d) * std_ref[pl.ds(start, size), :]

    lane = group_of((d.times, LANES), d)
    for h in range(d.halves):
        x = field_ref[pl.ds(h * d.group, d.times, stride=d.blocks), :]
        for m in range(1, d.group):
            x = jnp.where(lane == m, field_ref[pl.ds(h * d.group + m, d.times, stride=d.blocks), :], x)
        packed_ref[:, h * LANES:(h + 1) * LANES] = x


def unpack(d, packed, field_ref):
    lane = group_of((d.times, LANES), d)
    for h in range(d.halves):
        tile = packed[:, h * LANES:(h + 1) * LANES]
        for m in range(d.group):
            x = everywhere(jnp.where(lane == m, tile, 0.0), d)
            field_ref[pl.ds(h * d.group + m, d.times, stride=d.blocks), :] = x


def observe(d, mix_ref, packed_ref, rows_ref, place_ref, std_ref, field_ref, high_ref, low_ref, out_ref):
    unpack(d, dot3(mix_ref[...], packed_ref[...]), field_ref)
    size = CHUNK * d.blocks
    tail = 2 * CHUNK * d.blocks
    field_ref[pl.ds(d.times * d.blocks, tail), :] = jnp.zeros((tail, LANES), F32)

    @pl.loop(0, d.times // CHUNK)
    def _(i):
        start = pl.multiple_of(i * size, size)
        field_ref[pl.ds(start, size), :] = field_ref[pl.ds(start, size), :] * std_ref[pl.ds(start, size), :]

    lane = group_of((size, LANES), d)

    @pl.loop(0, d.times // CHUNK + 1)
    def _(i):
        start = pl.multiple_of(i * size, size)
        x = field_ref[pl.ds(start, size), :]
        for m in range(1, d.group):
            x = jnp.where(lane == m, field_ref[pl.ds(start + m * d.blocks, size), :], x)
        high, low = halves(x)
        high_ref[pl.ds(start, size), :] = high
        low_ref[pl.ds(start, size), :] = low

    for w in range(d.windows):
        starts = [(w * d.time_dev + d.group * g) * d.blocks for g in range(d.tiles)]
        high = jnp.concatenate([high_ref[s:s + d.places, :] for s in starts], axis=1)
        low = jnp.concatenate([low_ref[s:s + d.places, :] for s in starts], axis=1)
        place = place_ref[w]
        product = rows_ref[w].astype(F32) * (dot(place, high) + dot(place, low))
        part = product[:, :LANES]
        for g in range(1, d.tiles):
            part = part + product[:, g * LANES:(g + 1) * LANES]
        out_ref[w:w + 1, :] = jnp.sum(part.T, axis=0, keepdims=True)


def work_shapes(d):
    return [
        pltpu.VMEM(((FRONT + d.times + CHUNK) * d.blocks, LANES), F32),
        pltpu.VMEM(((d.times + 2 * CHUNK) * d.blocks, LANES), F32),
        pltpu.VMEM(((d.times + CHUNK) * d.blocks, LANES), BF16),
        pltpu.VMEM(((d.times + CHUNK) * d.blocks, LANES), BF16),
    ]


def in_order(d, me, x):
    block = iota(x.shape, 1)
    bit = 1
    while bit < d.windows:
        step = bit * d.chunk
        upper = (block // step) % 2 == 1
        other = jnp.where(upper, pltpu.roll(x, step, 1), pltpu.roll(x, d.slots - step, 1))
        x = jnp.where((me & bit) != 0, other, x)
        bit *= 2
    return x


def first_body(d, me_ref, mix_ref, *refs):
    got, refs = refs[:d.devices], refs[d.devices:]
    stds = refs[:d.windows]
    (rows_ref, place_t_ref, place_ref, std_ref, weight_ref, value_ref, packed_ref, seen_ref,
     wide_ref, stdp_ref, sum_ref, field_ref, high_ref, low_ref) = refs[d.windows:]
    me = me_ref[0]
    for s in range(d.devices):
        x = got[s][0:d.piece, :].astype(F32)
        source, low = me ^ (s // d.regions), s % d.regions * d.cap
        for w in range(d.windows):
            wide_ref[w, source, low:low + d.cap, :] = x[w * d.cap:(w + 1) * d.cap, :]
    for w in range(d.windows):
        for k in range(d.windows):
            rows_ref[w, k * d.chunk:(k + 1) * d.chunk] = wide_ref[w, k].astype(BF16)
    count = d.slots // LANES
    lane = iota((META, LANES), 1)
    meta = [[jnp.zeros((META, LANES), F32)] * count for _ in range(d.windows)]
    for s in range(d.devices):
        m = got[s][d.piece:d.rows, 0:LANES].astype(F32)
        low, high = s * d.cap, (s + 1) * d.cap
        for w in range(d.windows):
            turned = pltpu.roll(m, (low - w * d.cap) % LANES, 1)
            for tile in range(low // LANES, (high - 1) // LANES + 1):
                here = (lane + tile * LANES >= low) & (lane + tile * LANES < high)
                meta[w][tile] = jnp.where(here, turned, meta[w][tile])
    for w in range(d.windows):
        fields = in_order(d, me, jnp.concatenate(meta[w], axis=1))
        key = jnp.where(fields[6:7] > 0.5, fields[3:4] * d.blocks + fields[2:3], -1.0)
        number = key.astype(jnp.int32)
        place_t_ref[w] = onehot(iota((d.places, d.slots), 0) == jnp.broadcast_to(number, (d.places, d.slots)))
        column = transpose_rows(d, key).astype(jnp.int32)
        for k in range(d.places // LANES):
            place_ref[w, :, k * LANES:(k + 1) * LANES] = onehot(iota((d.slots, LANES), 1) + k * LANES == column)
        weight_ref[w:w + 1, :] = fields[4:5]
        value_ref[w:w + 1, :] = fields[4:5] * fields[5:6]
    for s in range(d.windows):
        stdp_ref[pl.ds(pl.multiple_of((me ^ s) * d.time_dev, 8), d.time_dev), :] = stds[s][...]
    unpack(d, stdp_ref[...], std_ref)
    spread(d, value_ref[...], rows_ref, place_t_ref, std_ref, sum_ref, field_ref, packed_ref)
    observe(d, mix_ref, packed_ref, rows_ref, place_ref, std_ref, field_ref, high_ref, low_ref, seen_ref)


def first(d, me, got, mix, stds):
    per_slot = jax.ShapeDtypeStruct((d.windows, d.slots), F32)
    return pl.pallas_call(
        functools.partial(first_body, d),
        name="first",
        in_specs=[smem()] + [vmem()] * (1 + d.devices + d.windows),
        out_specs=[vmem()] * 8,
        out_shape=[
            jax.ShapeDtypeStruct((d.windows, d.slots, d.width), BF16),
            jax.ShapeDtypeStruct((d.windows, d.places, d.slots), BF16),
            jax.ShapeDtypeStruct((d.windows, d.slots, d.places), BF16),
            jax.ShapeDtypeStruct((d.times * d.blocks, LANES), F32),
            per_slot,
            per_slot,
            jax.ShapeDtypeStruct((d.times, d.packed), F32),
            per_slot,
        ],
        scratch_shapes=[
            pltpu.VMEM((d.windows, d.windows, d.chunk, d.width), F32),
            pltpu.VMEM((d.times, d.packed), F32),
        ] + work_shapes(d),
        compiler_params=params(),
    )(me, mix, *got, *stds)


def total_of(x):
    return jnp.sum(jnp.sum(x, axis=0, keepdims=True), axis=1, keepdims=True)


def write_moments(out_ref, numbers):
    row = iota((8, LANES), 0)
    x = jnp.zeros((8, LANES), F32)
    for k, number in enumerate(numbers):
        x = jnp.where(row == k, jnp.broadcast_to(number, (8, LANES)), x)
    out_ref[...] = x


def second_body(d, rows_ref, place_t_ref, place_ref, std_ref, mix_ref, weight_ref, value_ref, *refs):
    parts = refs[:d.windows]
    (next_ref, packed_ref, seen_ref, moment_ref, sum_ref, field_ref, high_ref, low_ref) = refs[d.windows:]
    seen = parts[0][...]
    for p in parts[1:]:
        seen = seen + p[...]
    next_ref[...] = weight_ref[...] * seen
    write_moments(moment_ref, [total_of(value_ref[...] * seen), total_of(next_ref[...] * seen)])
    spread(d, next_ref[...], rows_ref, place_t_ref, std_ref, sum_ref, field_ref, packed_ref)
    observe(d, mix_ref, packed_ref, rows_ref, place_ref, std_ref, field_ref, high_ref, low_ref, seen_ref)


def second(d, rows, place_t, place, std, mix, weight, value, parts):
    per_slot = jax.ShapeDtypeStruct((d.windows, d.slots), F32)
    return pl.pallas_call(
        functools.partial(second_body, d),
        name="second",
        in_specs=[vmem()] * (7 + d.windows),
        out_specs=[vmem()] * 4,
        out_shape=[
            per_slot,
            jax.ShapeDtypeStruct((d.times, d.packed), F32),
            per_slot,
            jax.ShapeDtypeStruct((8, LANES), F32),
        ],
        scratch_shapes=work_shapes(d),
        compiler_params=params(),
    )(rows, place_t, place, std, mix, weight, value, *parts)


def third_body(d, weight_ref, value_ref, before_ref, *refs):
    parts = refs[:d.windows]
    next_ref, moment_ref = refs[d.windows:]
    seen = parts[0][...]
    for p in parts[1:]:
        seen = seen + p[...]
    next_ref[...] = weight_ref[...] * seen
    old = before_ref[...]
    write_moments(
        moment_ref,
        [old[0:1], old[1:2], total_of(value_ref[...] * seen), total_of(next_ref[...] * seen)],
    )


def third(d, weight, value, before, parts):
    return pl.pallas_call(
        functools.partial(third_body, d),
        name="third",
        in_specs=[vmem()] * (3 + d.windows),
        out_specs=[vmem()] * 2,
        out_shape=[
            jax.ShapeDtypeStruct((d.windows, d.slots), F32),
            jax.ShapeDtypeStruct((8, LANES), F32),
        ],
        compiler_params=params(),
    )(weight, value, before, *parts)


def fourth_body(d, value_ref, rows_ref, place_t_ref, std_ref, packed_ref, sum_ref, field_ref):
    spread(d, value_ref[...], rows_ref, place_t_ref, std_ref, sum_ref, field_ref, packed_ref)


def fourth(d, value, rows, place_t, std):
    return pl.pallas_call(
        functools.partial(fourth_body, d),
        name="fourth",
        in_specs=[vmem()] * 4,
        out_specs=vmem(),
        out_shape=jax.ShapeDtypeStruct((d.times, d.packed), F32),
        scratch_shapes=work_shapes(d)[:2],
        compiler_params=params(),
    )(value, rows, place_t, std)


def last_body(d, me_ref, moment_ref, factor_ref, a_ref, b_ref, c_ref, *refs):
    outs, hold_ref = refs[:d.windows], refs[d.windows]
    me = me_ref[0]
    m0, m1, m2, m3 = (moment_ref[k:k + 1, :] for k in range(4))
    alpha0 = m0 / (m0 + m1)
    p, q = 1.0 - alpha0, -alpha0
    norm = p * p * m0 + 2.0 * p * q * m1 + q * q * m2
    e = p + norm / m0
    cross = (e * e * m0 + 2.0 * e * q * m1 + q * q * m2) + (e * e * m1 + 2.0 * e * q * m2 + q * q * m3)
    alpha1 = norm / cross
    for h in range(d.halves):
        low, high = h * LANES, (h + 1) * LANES
        a, b, c = a_ref[:, low:high], b_ref[:, low:high], c_ref[:, low:high]
        x = (alpha0 + alpha1 * e) * a + (alpha1 * q) * b
        r = (p - alpha1 * e) * a + (q - alpha1 * (e + q)) * b - (alpha1 * q) * c
        for k, v in enumerate((x, r)):
            fh, fl = halves(factor_ref[...])
            vh, vl = halves(v)
            y = dot(fh, vh, (0, 0)) + (dot(fh, vl, (0, 0)) + dot(fl, vh, (0, 0)))
            hold_ref[k, :, low:high] = y
    for s in range(d.windows):
        start = pl.multiple_of((me ^ s) * d.time_dev, 8)
        for k in range(2):
            outs[s][k] = hold_ref[k, pl.ds(start, d.time_dev), :]


def last(d, me, moments, factor, a, b, c):
    return pl.pallas_call(
        functools.partial(last_body, d),
        name="last",
        in_specs=[smem()] + [vmem()] * 5,
        out_specs=[vmem()] * d.windows,
        out_shape=[jax.ShapeDtypeStruct((2, d.time_dev, d.packed), F32)] * d.windows,
        scratch_shapes=[pltpu.VMEM((2, d.times, d.packed), F32)],
        compiler_params=params(),
    )(me, moments, factor, a, b, c)


def swap(x, axis, step):
    size = lax.axis_size(axis)
    return lax.ppermute(x, axis, [(k, k ^ step) for k in range(size)])


def share(d, x):
    return [x] + [swap(x, "tm", s) for s in range(1, d.windows)]


def local(
    jacobian,
    foot_block,
    foot_time,
    obs_weight,
    misfit,
    kept_list,
    kept_count,
    prior_std,
    time_factor,
):
    d = Dims(jacobian, kept_list, prior_std, lax.axis_size("region"), lax.axis_size("tm"))
    me = lax.axis_index("tm").astype(jnp.int32).reshape(1)
    mix = jnp.dot(time_factor, time_factor.T, precision=lax.Precision.HIGHEST)
    ours = split_prior(d, me, prior_std)
    stds = [ours[0]] + [swap(ours[s], "tm", s) for s in range(1, d.windows)]
    row = lax.axis_index("region").astype(jnp.int32).reshape(1)
    sliced = slice_rows(d, me, kept_count, kept_list, foot_block, foot_time, obs_weight, misfit, jacobian)
    near = [sliced[0]] + [swap(sliced[s], "tm", s) for s in range(1, d.windows)]
    got = []
    for piece in near:
        routed = route(d, row, piece)
        got += [routed[0]] + [swap(routed[x], "region", x) for x in range(1, d.regions)]
    rows, place_t, place, std, weight, value0, u0, seen0 = first(d, me, got, mix, stds)
    value1, u1, seen1, early = second(d, rows, place_t, place, std, mix, weight, value0, share(d, seen0))
    value2, moments = third(d, weight, value1, early, share(d, seen1))
    u2 = fourth(d, value2, rows, place_t, std)
    step = 1
    while step < d.regions:
        moments = moments + swap(moments, "region", step)
        step *= 2
    both = last(d, me, moments, time_factor, u0, u1, u2)
    parts = [both[0]] + [swap(both[s], "tm", s) for s in range(1, d.windows)]
    return join(d, me, parts)


def solution(mesh):
    return jax.shard_map(
        local,
        mesh=mesh,
        in_specs=(
            P(("region", "tm"), None),
            P(("region", "tm")),
            P(("region", "tm")),
            P(("region", "tm")),
            P(("region", "tm")),
            P(("region", "tm")),
            P(("region", "tm")),
            P("tm", "region", None),
            P(),
        ),
        out_specs=(P("tm", "region", None), P("tm", "region", None)),
        check_vma=False,
    )
```

```python
import functools

import jax
import jax.numpy as jnp
from jax import lax
from jax.experimental import pallas as pl
from jax.experimental.pallas import tpu as pltpu
from jax.sharding import PartitionSpec as P


F32 = jnp.float32
BF16 = jnp.bfloat16
LANES = 128
VMEM_LIMIT = 40 << 20
META = 8


class Dims:
    def __init__(self, jacobian, kept_list, prior_std, regions, windows):
        self.regions = regions
        self.windows = windows
        self.devices = regions * windows
        self.time_dev, self.blocks, self.cells = prior_std.shape
        self.pool = jacobian.shape[0]
        self.keep = kept_list.shape[0]
        self.lag = jacobian.shape[1] // self.cells
        self.times = self.time_dev * windows
        self.cap = 3 * self.keep // (2 * self.devices)
        self.slice = self.cells // windows
        self.group = LANES // self.slice
        self.tiles = self.lag // self.group
        self.width = self.lag * self.slice
        self.slots = self.devices * self.cap
        self.piece = windows * self.cap
        self.chunk = regions * self.cap
        self.late = (windows - 1) * self.chunk
        self.cut = self.late // LANES * LANES
        self.rows = self.piece + META
        self.ahead = self.tiles // 2
        self.head = META * (self.keep // (self.ahead * LANES))
        self.offsets = -(-(self.time_dev - self.lag + 1) // 16) * 16
        self.places = self.offsets * self.blocks
        self.halves = self.blocks // self.group
        self.packed = self.halves * LANES
        assert self.cells == LANES and self.blocks == 8 and self.group == windows


def iota(shape, axis):
    return lax.broadcasted_iota(jnp.int32, shape, axis)


def onehot(match):
    return jnp.where(match, 1.0, 0.0).astype(BF16)


def dot(a, b, contract=(1, 0)):
    return lax.dot_general(
        a, b, (((contract[0],), (contract[1],)), ((), ())), preferred_element_type=F32
    )


def halves(x):
    high = x.astype(BF16)
    return high, (x - high.astype(F32)).astype(BF16)


def thirds(x):
    high, rest = x.astype(BF16), x - x.astype(BF16).astype(F32)
    return (high, *halves(rest))


def dot3(a, b):
    ah, al = halves(a)
    bh, bl = halves(b)
    return dot(ah, bh) + (dot(ah, bl) + dot(al, bh))


def group_of(shape, d):
    return iota(shape, 1) >> (d.slice.bit_length() - 1)


def params(limit=VMEM_LIMIT):
    return pltpu.CompilerParams(vmem_limit_bytes=limit)


def vmem():
    return pl.BlockSpec(memory_space=pltpu.VMEM)


def smem():
    return pl.BlockSpec(memory_space=pltpu.SMEM)


def turn_matrix(d, me):
    wide = d.group * LANES
    a, b = iota((wide, wide), 0), iota((wide, wide), 1)
    bits = d.slice.bit_length() - 1
    cell = a & (LANES - 1)
    place = (((cell >> bits) ^ me) << 7) + ((a >> 7) << bits) + (cell & (d.slice - 1))
    return onehot(place == b)


def slice_body(d, with_meta, me_ref, count_ref, list_ref, block_ref, time_ref, weight_ref, misfit_ref, jac_ref,
               *refs):
    outs, (select_ref, meta_ref, turn_ref) = refs[:d.windows], refs[d.windows:]
    step = pl.program_id(0)

    @pl.when(step == 0)
    def _():
        listed = jnp.broadcast_to(list_ref[...].astype(F32)[None], (LANES, d.keep)).T.astype(jnp.int32)
        for k in range(d.pool // LANES):
            select_ref[:, k * LANES:(k + 1) * LANES] = onehot(iota((d.keep, LANES), 1) + k * LANES == listed)
        turn_ref[...] = turn_matrix(d, me_ref[0])
        if with_meta:
            block = block_ref[...][None]
            time = time_ref[...][None]
            window = jnp.zeros_like(time)
            for w in range(1, d.windows):
                window += jnp.where(time >= w * d.time_dev, 1, 0)
            row = iota((16, d.pool), 0)
            fields = jnp.where(row == 0, (block >> 3).astype(F32), 0.0)
            fields = jnp.where(row == 1, window.astype(F32), fields)
            fields = jnp.where(row == 2, (block & 7).astype(F32), fields)
            fields = jnp.where(row == 3, (time - window * d.time_dev).astype(F32), fields)
            fields = jnp.where(row == 4, weight_ref[...].astype(F32)[None], fields)
            fields = jnp.where(row == 5, misfit_ref[...].astype(F32)[None], fields)
            fields = dot(fields.astype(BF16), select_ref[...], (1, 1))[0:META]
            live = (iota((META, d.keep), 1) < count_ref[0]) & (iota((META, d.keep), 0) == 6)
            meta_ref[...] = jnp.where(live, 1.0, fields).astype(BF16)

    rows = dot(select_ref[...], jac_ref[...]).astype(BF16)
    turned = dot(rows, turn_ref[...]).astype(BF16)
    for s in range(d.windows):
        outs[s][0:d.keep, :] = turned[:, s * LANES:(s + 1) * LANES]
    if with_meta:
        per = d.keep // d.ahead
        for g in range(d.ahead):
            @pl.when(step == g)
            def _():
                meta = meta_ref[:, g * per:(g + 1) * per]
                for s in range(d.windows):
                    outs[s][d.keep:d.keep + d.head, :] = jnp.concatenate(
                        [meta[:, k * LANES:(k + 1) * LANES] for k in range(per // LANES)], axis=0
                    )


def slice_rows(d, ahead, me, count, listed, block, time, weight, misfit, jacobian):
    wide = d.group * LANES
    whole = lambda n: pl.BlockSpec((n,), lambda g: (0,))
    first, tiles = (0, d.ahead) if ahead else (d.ahead, d.tiles - d.ahead)
    rows = d.keep + (d.head if ahead else 0)
    return pl.pallas_call(
        functools.partial(slice_body, d, ahead),
        name="slice_rows",
        grid=(tiles,),
        in_specs=[smem(), smem(), whole(d.keep)] + [whole(d.pool)] * 4
        + [pl.BlockSpec((d.pool, wide), lambda g: (0, g + first))],
        out_specs=[pl.BlockSpec((rows, LANES), lambda g: (0, g))] * d.windows,
        out_shape=[jax.ShapeDtypeStruct((rows, tiles * LANES), BF16)] * d.windows,
        scratch_shapes=[
            pltpu.VMEM((d.keep, d.pool), BF16),
            pltpu.VMEM((META, d.keep), BF16),
            pltpu.VMEM((wide, wide), BF16),
        ],
        compiler_params=params(60 << 20),
    )(me, count, listed, block, time, weight, misfit, jacobian)


def selection(d, row, in_ref):
    per = d.head // META
    meta = jnp.concatenate(
        [in_ref[d.keep + META * k:d.keep + META * (k + 1), g * LANES:(g + 1) * LANES]
         for g in range(d.ahead) for k in range(per)],
        axis=1,
    )
    fields = meta.astype(F32)
    region = fields[0:1].astype(jnp.int32) ^ row
    target = region * d.windows + fields[1:2].astype(jnp.int32)
    target = jnp.where(fields[6:7] > 0.5, target, -1)
    mine = iota((d.devices, d.keep), 0) == jnp.broadcast_to(target, (d.devices, d.keep))
    before = onehot(iota((d.keep, d.keep), 0) < iota((d.keep, d.keep), 1))
    ranks = dot(onehot(mine), before)
    rank = jnp.sum(jnp.where(mine, ranks, 0.0), axis=0, keepdims=True).astype(jnp.int32)
    slot = jnp.where(target >= 0, target * d.cap + rank, -1)
    return meta, onehot(iota((d.slots, d.keep), 0) == jnp.broadcast_to(slot, (d.slots, d.keep)))


def route_body(d, row_ref, part_a_ref, part_b_ref, *outs):
    parts = (part_a_ref, part_b_ref)
    meta, select = selection(d, row_ref[0], part_a_ref)
    placed = dot(jnp.concatenate([meta, meta], axis=0), select, (1, 1))[0:META]
    low = 0
    for part in parts:
        packed = dot(select, part[0:d.keep, :]).astype(BF16)
        high = low + packed.shape[1]
        for r in range(d.regions):
            outs[r][0:d.piece, low:high] = packed[r * d.piece:(r + 1) * d.piece]
        low = high
    for r in range(d.regions):
        shifted = pltpu.roll(placed, (d.slots - r * d.piece) % d.slots, 1)[:, :LANES]
        outs[r][d.piece:d.rows, 0:LANES] = shifted.astype(BF16)
        if low > LANES:
            outs[r][d.piece:d.rows, LANES:] = jnp.zeros((META, low - LANES), BF16)


def route(d, row, part_a, part_b):
    return pl.pallas_call(
        functools.partial(route_body, d),
        name="route",
        in_specs=[smem(), vmem(), vmem()],
        out_specs=[vmem()] * d.regions,
        out_shape=[jax.ShapeDtypeStruct((d.rows, d.width), BF16)] * d.regions,
        compiler_params=params(),
    )(row, part_a, part_b)


def prior_body(d, me_ref, prior_ref, *outs):
    me = me_ref[0]
    lane = group_of((d.time_dev, LANES), d)
    for h in range(d.halves):
        rows = [prior_ref[pl.ds(h * d.group + m, d.time_dev, stride=d.blocks), :] for m in range(d.group)]
        for s in range(d.windows):
            to = me ^ s
            total = jnp.zeros((d.time_dev, LANES), F32)
            for m in range(d.group):
                turn = (m - to + d.group) % d.group * d.slice
                total = jnp.where(lane == m, pltpu.roll(rows[m], turn, 1), total)
            outs[s][:, h * LANES:(h + 1) * LANES] = total


def split_prior(d, me, prior):
    return pl.pallas_call(
        functools.partial(prior_body, d),
        name="split_prior",
        in_specs=[smem(), vmem()],
        out_specs=[vmem()] * d.windows,
        out_shape=[jax.ShapeDtypeStruct((d.time_dev, d.packed), F32)] * d.windows,
        compiler_params=params(),
    )(me, prior.reshape(d.time_dev * d.blocks, LANES))


FRONT = 8
CHUNK = 16


def set_places(d, key, place_t_ref, place_ref, w):
    count = key.shape[1]
    number = jnp.broadcast_to(key.astype(jnp.int32), (d.places, count))
    place_t_ref[w] = onehot(iota((d.places, count), 0) == number)
    column = jnp.broadcast_to(key, (LANES, count)).T.astype(jnp.int32)
    for k in range(d.places // LANES):
        hit = onehot(iota((count, LANES), 1) + k * LANES == column)
        place_ref[w, :, k * LANES:(k + 1) * LANES] = hit
        place_ref[w, :, d.places + k * LANES:d.places + (k + 1) * LANES] = hit


def unite_rows(d, got, base, wide_ref):
    for k, ref in enumerate(got):
        x = ref[0:d.piece, :].astype(F32)
        s = base + k
        for w in range(d.windows):
            wide_ref[w, s * d.cap:(s + 1) * d.cap, :] = x[w * d.cap:(w + 1) * d.cap, :]


def unite_meta(d, got, base):
    lane = iota((META, LANES), 1)
    meta = [[jnp.zeros((META, LANES), F32)] * (d.slots // LANES) for _ in range(d.windows)]
    for k, ref in enumerate(got):
        m = ref[d.piece:d.rows, 0:LANES].astype(F32)
        low, high = (base + k) * d.cap, (base + k + 1) * d.cap
        for w in range(d.windows):
            turned = pltpu.roll(m, (low - w * d.cap) % LANES, 1)
            for tile in range(low // LANES, (high - 1) // LANES + 1):
                here = (lane + tile * LANES >= low) & (lane + tile * LANES < high)
                meta[w][tile] = jnp.where(here, turned, meta[w][tile])
    rows = []
    for w in range(d.windows):
        fields = jnp.concatenate(meta[w], axis=1)
        key = jnp.where(fields[6:7] > 0.5, fields[3:4] * d.blocks + fields[2:3], -1.0)
        rows.append((key, fields[4:5], fields[4:5] * fields[5:6]))
    return rows


def add_rows(d, values, low, rows_ref, place_t_ref, sum_ref):
    for w in range(d.windows):
        rows, place = rows_ref[w], place_t_ref[w]
        high_part, low_part = halves(values[w:w + 1, low:low + rows.shape[0]])
        total = dot(jnp.concatenate([place * high_part, place * low_part], axis=0), rows)
        total = total[:d.places] + total[d.places:]
        for g in range(d.tiles):
            start = (FRONT + w * d.time_dev + d.group * g) * d.blocks
            sum_ref[start:start + d.places, :] += total[:, g * LANES:(g + 1) * LANES]


def spread(d, values, slots, std_ref, sum_ref, packed_ref):
    sum_ref[...] = jnp.zeros_like(sum_ref)
    for low, rows_ref, place_t_ref, _ in slots:
        add_rows(d, values, low, rows_ref, place_t_ref, sum_ref)
    finish(d, std_ref, sum_ref, packed_ref)


def finish(d, std_ref, sum_ref, packed_ref):
    size = d.time_dev
    lane = group_of((size, LANES), d)
    for h in range(d.halves):
        for start in range(0, d.times, size):
            total = None
            for k in range(d.group):
                x = None
                for m in range(d.group):
                    block = h * d.group + (m - k) % d.group
                    row = (FRONT + start - m) * d.blocks + block
                    y = sum_ref[pl.ds(row, size, stride=d.blocks), :]
                    x = y if x is None else jnp.where(lane == m, y, x)
                if k:
                    x = pltpu.roll(x, LANES - k * d.slice, 1)
                total = x if total is None else total + x
            here = (slice(start, start + size), slice(h * LANES, (h + 1) * LANES))
            packed_ref[here] = total * std_ref[here]


def observe(d, mix_ref, packed_ref, slots, std_ref, turn_ref, field_ref, high_ref, low_ref, out_ref):
    packed = dot3(mix_ref[...], packed_ref[...]) * std_ref[...]
    for h in range(d.halves):
        tile = packed[:, h * LANES:(h + 1) * LANES]
        for k in range(d.group):
            turn = pltpu.roll(tile, k * d.slice, 1) if k else tile
            turn_ref[h * d.group + k, 0:d.times, :] = turn
            turn_ref[h * d.group + k, d.times:, :] = jnp.zeros((2 * CHUNK, LANES), F32)
    lane = group_of((CHUNK, LANES), d)
    for start in range(0, d.times + CHUNK, CHUNK):
        for block in range(d.blocks):
            h, m = divmod(block, d.group)
            x = None
            for q in range(d.group):
                y = turn_ref[h * d.group + (q - m) % d.group, start + q:start + q + CHUNK, :]
                x = y if x is None else jnp.where(lane == q, y, x)
            field_ref[pl.ds(start * d.blocks + block, CHUNK, stride=d.blocks), :] = x
        here = slice(start * d.blocks, (start + CHUNK) * d.blocks)
        high_ref[here, :], low_ref[here, :] = halves(field_ref[here, :])

    for w in range(d.windows):
        starts = [(w * d.time_dev + d.group * g) * d.blocks for g in range(d.tiles)]
        both = jnp.concatenate(
            [jnp.concatenate([ref[s:s + d.places, :] for s in starts], axis=1) for ref in (high_ref, low_ref)], axis=0
        )
        for first, rows_ref, _, place_ref in slots:
            rows, place = rows_ref[w], place_ref[w]
            product = rows.astype(F32) * dot(place, both)
            part = product[:, :LANES]
            for g in range(1, d.tiles):
                part = part + product[:, g * LANES:(g + 1) * LANES]
            out_ref[w:w + 1, first:first + rows.shape[0]] = jnp.sum(part.T, axis=0, keepdims=True)


def work_shapes(d):
    return [
        pltpu.VMEM(sum_shape(d), F32),
        pltpu.VMEM((d.blocks, d.times + 2 * CHUNK, LANES), F32),
        pltpu.VMEM(((d.times + CHUNK) * d.blocks, LANES), F32),
        pltpu.VMEM(((d.times + CHUNK) * d.blocks, LANES), BF16),
        pltpu.VMEM(((d.times + CHUNK) * d.blocks, LANES), BF16),
    ]


def from_peer(d, step, x):
    place = iota(x.shape, 1)
    chunk = jnp.zeros_like(place)
    for k in range(1, d.windows):
        chunk += jnp.where(place >= k * d.chunk, 1, 0)
    bit = 1
    while bit <= step:
        if step & bit:
            move = bit * d.chunk
            x = jnp.where((chunk & bit) != 0, pltpu.roll(x, move, 1), pltpu.roll(x, d.slots - move, 1))
        bit *= 2
    return x


def add_peers(d, parts):
    seen = parts[0][...]
    for step in range(1, d.windows):
        seen = seen + from_peer(d, step, parts[step][...])
    return seen


def early_body(d, *refs):
    n = (d.windows - 1) * d.regions
    got = refs[:n]
    (rows_ref, rest_ref, place_t_ref, place_ref, key_ref, weight_ref, value_ref, sum_ref, wide_ref) = refs[n:]
    unite_rows(d, got, 0, wide_ref)
    for w in range(d.windows):
        rows_ref[w] = wide_ref[w, 0:d.cut].astype(BF16)
        rest_ref[w] = wide_ref[w, d.cut:d.late].astype(BF16)
    for w, (key, weight, value) in enumerate(unite_meta(d, got, 0)):
        set_places(d, key[:, :d.cut], place_t_ref, place_ref, w)
        key_ref[w:w + 1, :] = key
        weight_ref[w:w + 1, :] = weight
        value_ref[w:w + 1, :] = value
    sum_ref[...] = jnp.zeros_like(sum_ref)
    add_rows(d, value_ref[...], 0, rows_ref, place_t_ref, sum_ref)


def sum_shape(d):
    return ((FRONT + d.times + CHUNK) * d.blocks, LANES)


def early(d, got):
    per_slot = jax.ShapeDtypeStruct((d.windows, d.slots), F32)
    return pl.pallas_call(
        functools.partial(early_body, d),
        name="early",
        in_specs=[vmem()] * len(got),
        out_specs=[vmem()] * 8,
        out_shape=[
            jax.ShapeDtypeStruct((d.windows, d.cut, d.width), BF16),
            jax.ShapeDtypeStruct((d.windows, d.late - d.cut, d.width), BF16),
            jax.ShapeDtypeStruct((d.windows, d.places, d.cut), BF16),
            jax.ShapeDtypeStruct((d.windows, d.cut, 2 * d.places), BF16),
            per_slot,
            per_slot,
            per_slot,
            jax.ShapeDtypeStruct(sum_shape(d), F32),
        ],
        scratch_shapes=[pltpu.VMEM((d.windows, d.late, d.width), F32)],
        compiler_params=params(),
    )(*got)


def late_body(d, rest_ref, key_ref, weight_a_ref, value_a_ref, sum_a_ref, *refs):
    got, refs = refs[:d.regions], refs[d.regions:]
    rows_ref, place_t_ref, place_ref, weight_ref, value_ref, sum_ref, wide_ref = refs
    new = iota((1, d.slots), 1) >= d.late
    for w, (key, weight, value) in enumerate(unite_meta(d, got, d.late // d.cap)):
        key = jnp.where(new, key, key_ref[w:w + 1, :])
        set_places(d, key[:, d.cut:], place_t_ref, place_ref, w)
        weight_ref[w:w + 1, :] = jnp.where(new, weight, weight_a_ref[w:w + 1, :])
        value_ref[w:w + 1, :] = jnp.where(new, value, value_a_ref[w:w + 1, :])
    unite_rows(d, got, 0, wide_ref)
    for w in range(d.windows):
        rows_ref[w, 0:d.late - d.cut] = rest_ref[w]
        rows_ref[w, d.late - d.cut:] = wide_ref[w].astype(BF16)
    sum_ref[...] = sum_a_ref[...]
    add_rows(d, value_ref[...], d.cut, rows_ref, place_t_ref, sum_ref)


def late(d, rest, key, weight, value, total, got):
    per_slot = jax.ShapeDtypeStruct((d.windows, d.slots), F32)
    tail = d.slots - d.cut
    return pl.pallas_call(
        functools.partial(late_body, d),
        name="late",
        in_specs=[vmem()] * (5 + d.regions),
        out_specs=[vmem()] * 6,
        out_shape=[
            jax.ShapeDtypeStruct((d.windows, tail, d.width), BF16),
            jax.ShapeDtypeStruct((d.windows, d.places, tail), BF16),
            jax.ShapeDtypeStruct((d.windows, tail, 2 * d.places), BF16),
            per_slot,
            per_slot,
            jax.ShapeDtypeStruct(sum_shape(d), F32),
        ],
        scratch_shapes=[pltpu.VMEM((d.windows, d.chunk, d.width), F32)],
        compiler_params=params(),
    )(rest, key, weight, value, total, *got)


def first_body(d, me_ref, mix_ref, sum_ref, *refs):
    slots, refs = slots_of(d, refs[:6]), refs[6:]
    stds = refs[:d.windows]
    std_ref, packed_ref, seen_ref, *work = refs[d.windows:]
    for s in range(d.windows):
        std_ref[pl.ds(pl.multiple_of((me_ref[0] ^ s) * d.time_dev, 8), d.time_dev), :] = stds[s][...]
    finish(d, std_ref, sum_ref, packed_ref)
    observe(d, mix_ref, packed_ref, slots, std_ref, *work, seen_ref)


def first(d, me, mix, total, slots, stds):
    return pl.pallas_call(
        functools.partial(first_body, d),
        name="first",
        in_specs=[smem()] + [vmem()] * (8 + d.windows),
        out_specs=[vmem()] * 3,
        out_shape=[
            jax.ShapeDtypeStruct((d.times, d.packed), F32),
            jax.ShapeDtypeStruct((d.times, d.packed), F32),
            jax.ShapeDtypeStruct((d.windows, d.slots), F32),
        ],
        scratch_shapes=work_shapes(d)[1:],
        compiler_params=params(),
    )(me, mix, total, *slots, *stds)


def slots_of(d, refs):
    return [(0, *refs[:3]), (d.cut, *refs[3:])]


def total_of(x):
    return jnp.sum(jnp.sum(x, axis=0, keepdims=True), axis=1, keepdims=True)


def write_moments(out_ref, numbers):
    row = iota((8, LANES), 0)
    x = jnp.zeros((8, LANES), F32)
    for k, number in enumerate(numbers):
        x = jnp.where(row == k, jnp.broadcast_to(number, (8, LANES)), x)
    out_ref[...] = x


def second_body(d, *refs):
    slots, refs = slots_of(d, refs[:6]), refs[6:]
    (std_ref, mix_ref, weight_ref, value_ref), refs = refs[:4], refs[4:]
    parts = refs[:d.windows]
    (next_ref, packed_ref, seen_ref, moment_ref, sum_ref, *work) = refs[d.windows:]
    seen = add_peers(d, parts)
    next_ref[...] = weight_ref[...] * seen
    write_moments(moment_ref, [total_of(value_ref[...] * seen), total_of(next_ref[...] * seen)])
    spread(d, next_ref[...], slots, std_ref, sum_ref, packed_ref)
    observe(d, mix_ref, packed_ref, slots, std_ref, *work, seen_ref)


def second(d, slots, std, mix, weight, value, parts):
    per_slot = jax.ShapeDtypeStruct((d.windows, d.slots), F32)
    return pl.pallas_call(
        functools.partial(second_body, d),
        name="second",
        in_specs=[vmem()] * (10 + d.windows),
        out_specs=[vmem()] * 4,
        out_shape=[
            per_slot,
            jax.ShapeDtypeStruct((d.times, d.packed), F32),
            per_slot,
            jax.ShapeDtypeStruct((8, LANES), F32),
        ],
        scratch_shapes=work_shapes(d),
        compiler_params=params(),
    )(*slots, std, mix, weight, value, *parts)


def third_body(d, weight_ref, value_ref, before_ref, *refs):
    parts = refs[:d.windows]
    next_ref, moment_ref = refs[d.windows:]
    seen = add_peers(d, parts)
    next_ref[...] = weight_ref[...] * seen
    old = before_ref[...]
    write_moments(
        moment_ref,
        [old[0:1], old[1:2], total_of(value_ref[...] * seen), total_of(next_ref[...] * seen)],
    )


def third(d, weight, value, before, parts):
    return pl.pallas_call(
        functools.partial(third_body, d),
        name="third",
        in_specs=[vmem()] * (3 + d.windows),
        out_specs=[vmem()] * 2,
        out_shape=[
            jax.ShapeDtypeStruct((d.windows, d.slots), F32),
            jax.ShapeDtypeStruct((8, LANES), F32),
        ],
        compiler_params=params(),
    )(weight, value, before, *parts)


def by_window(d, me, k, factor_ref, packed, hold_ref, outs):
    f, v = thirds(factor_ref[...]), thirds(packed)
    small = dot(f[0], v[2], (0, 0)) + dot(f[1], v[1], (0, 0)) + dot(f[2], v[0], (0, 0))
    hold_ref[...] = dot(f[0], v[0], (0, 0)) + (dot(f[0], v[1], (0, 0)) + dot(f[1], v[0], (0, 0)) + small)
    for s in range(d.windows):
        start = pl.multiple_of((me ^ s) * d.time_dev, 8)
        outs[s][k] = hold_ref[pl.ds(start, d.time_dev), :]


def results_body(d, me_ref, factor_ref, *refs):
    n = len(refs) - 1 - d.windows
    outs, hold_ref = refs[n:n + d.windows], refs[-1]
    for k in range(n):
        by_window(d, me_ref[0], k, factor_ref, refs[k][...], hold_ref, outs)


def results(d, me, factor, packed):
    return pl.pallas_call(
        functools.partial(results_body, d),
        name="results",
        in_specs=[smem()] + [vmem()] * (1 + len(packed)),
        out_specs=[vmem()] * d.windows,
        out_shape=[jax.ShapeDtypeStruct((len(packed), d.time_dev, d.packed), F32)] * d.windows,
        scratch_shapes=[pltpu.VMEM((d.times, d.packed), F32)],
        compiler_params=params(),
    )(me, factor, *packed)


def fourth_body(d, me_ref, factor_ref, value_ref, std_ref, *refs):
    slots, refs = slots_of(d, refs[:6]), refs[6:]
    outs = refs[:d.windows]
    packed_ref, hold_ref, sum_ref = refs[d.windows:]
    spread(d, value_ref[...], slots, std_ref, sum_ref, packed_ref)
    by_window(d, me_ref[0], 0, factor_ref, packed_ref[...], hold_ref, outs)


def fourth(d, me, factor, value, std, slots):
    return pl.pallas_call(
        functools.partial(fourth_body, d),
        name="fourth",
        in_specs=[smem()] + [vmem()] * 9,
        out_specs=[vmem()] * d.windows,
        out_shape=[jax.ShapeDtypeStruct((1, d.time_dev, d.packed), F32)] * d.windows,
        scratch_shapes=[pltpu.VMEM((d.times, d.packed), F32)] * 2 + work_shapes(d)[:1],
        compiler_params=params(),
    )(me, factor, value, std, *slots)


def join_body(d, me_ref, moment_ref, *refs):
    two, one, outs = refs[:d.windows], refs[d.windows:2 * d.windows], refs[2 * d.windows:]
    me = me_ref[0]
    m0, m1, m2, m3 = (moment_ref[k:k + 1, :] for k in range(4))
    alpha0 = m0 / (m0 + m1)
    p, q = 1.0 - alpha0, -alpha0
    norm = p * p * m0 + 2.0 * p * q * m1 + q * q * m2
    e = p + norm / m0
    cross = (e * e * m0 + 2.0 * e * q * m1 + q * q * m2) + (e * e * m1 + 2.0 * e * q * m2 + q * q * m3)
    alpha1 = norm / cross
    lane = group_of((d.time_dev, LANES), d)
    for h in range(d.halves):
        low, high = h * LANES, (h + 1) * LANES
        tiles = [[], []]
        for s in range(d.windows):
            a, b, c = two[s][0, :, low:high], two[s][1, :, low:high], one[s][0, :, low:high]
            tiles[0].append((alpha0 + alpha1 * e) * a + (alpha1 * q) * b)
            tiles[1].append((p - alpha1 * e) * a + (q - alpha1 * (e + q)) * b - (alpha1 * q) * c)
        for k in range(2):
            for m in range(d.group):
                total = jnp.zeros((d.time_dev, LANES), F32)
                for s in range(d.windows):
                    source = me ^ s
                    turn = (source - m + d.group) % d.group * d.slice
                    total = jnp.where(lane == source, pltpu.roll(tiles[k][s], turn, 1), total)
                outs[k][pl.ds(h * d.group + m, d.time_dev, stride=d.blocks), :] = total


def join(d, me, moments, two, one):
    flat = jax.ShapeDtypeStruct((d.time_dev * d.blocks, LANES), F32)
    outs = pl.pallas_call(
        functools.partial(join_body, d),
        name="join",
        in_specs=[smem()] + [vmem()] * (1 + 2 * d.windows),
        out_specs=[vmem()] * 2,
        out_shape=[flat, flat],
        compiler_params=params(),
    )(me, moments, *two, *one)
    return tuple(o.reshape(d.time_dev, d.blocks, LANES) for o in outs)


def swap(x, axis, step):
    size = lax.axis_size(axis)
    return lax.ppermute(x, axis, [(k, k ^ step) for k in range(size)])


def share(d, x):
    return [x] + [swap(x, "tm", s) for s in range(1, d.windows)]


def deal(parts):
    return [parts[0]] + [swap(parts[s], "tm", s) for s in range(1, len(parts))]


def program(
    jacobian, foot_block, foot_time, obs_weight, misfit, kept_list, kept_count, prior_std, time_factor
):
    d = Dims(jacobian, kept_list, prior_std, lax.axis_size("region"), lax.axis_size("tm"))
    me = lax.axis_index("tm").astype(jnp.int32).reshape(1)
    row = lax.axis_index("region").astype(jnp.int32).reshape(1)
    mix = jnp.dot(time_factor, time_factor.T, precision=lax.Precision.HIGHEST)
    listed = (me, kept_count, kept_list, foot_block, foot_time, obs_weight, misfit, jacobian)
    sliced = slice_rows(d, True, *listed)
    near_a = deal(sliced[:-1])
    sliced_b = slice_rows(d, False, *listed)
    near_b = deal(sliced_b[:-1])
    near_a.append(swap(sliced[-1], "tm", d.windows - 1))
    near_b.append(swap(sliced_b[-1], "tm", d.windows - 1))
    ours = split_prior(d, me, prior_std)

    def send(pieces):
        return [pieces[0]] + [swap(pieces[x], "region", x) for x in range(1, d.regions)]

    got = []
    for s in range(d.windows):
        routed = route(d, row, near_a[s], near_b[s])
        got.append(send(routed))
    stds = deal(ours)
    rows_a, rest, place_t_a, place_a, key, weight, value0, total = early(d, sum(got[:-1], []))
    rows_b, place_t_b, place_b, weight, value0, total = late(d, rest, key, weight, value0, total, got[-1])
    slots = (rows_a, place_t_a, place_a, rows_b, place_t_b, place_b)
    std, u0, seen0 = first(d, me, mix, total, slots, stds)
    parts = share(d, seen0)
    value1, u1, seen1, moments = second(d, slots, std, mix, weight, value0, parts)
    parts = share(d, seen1)
    both = results(d, me, time_factor, [u0, u1])
    two = deal(both)
    value2, moments = third(d, weight, value1, moments, parts)
    for k in range(d.regions.bit_length() - 1):
        moments = moments + swap(moments, "region", 1 << k)
    last = fourth(d, me, time_factor, value2, std, slots)
    one = deal(last)
    return join(d, me, moments, two, one)


def solution(mesh):
    return jax.shard_map(
        program,
        mesh=mesh,
        in_specs=(
            P(("region", "tm"), None),
            P(("region", "tm")),
            P(("region", "tm")),
            P(("region", "tm")),
            P(("region", "tm")),
            P(("region", "tm")),
            P(("region", "tm")),
            P("tm", "region", None),
            P(),
        ),
        out_specs=(P("tm", "region", None), P("tm", "region", None)),
        check_vma=False,
    )
```
